512 devices in a mesh: src: 16 (over z), tile: 8 (over x, core), gauge: 4 (over y).
Axes of the slice: x: 4, y: 4, z: 16, core: 2. Of those that a mesh axis runs over, the one named last changes fastest.
Arguments:
- responses: float32 [512, 2, 4, 128, 256], P(('src', 'tile'), None, 'gauge'), may hold values from -0.1875 to 0.1875
- footprint: int32 [512, 2], P(('src', 'tile')), may hold values from 0 to 15, all different within a row; in each aligned block of 4 rows (0 to 3, 4 to 7, ...) at most 2 rows name the same one
- theta_start: float32 [512, 8, 128], P(('src', 'tile')), may hold values from -4 to 4
- observed: float32 [128, 4, 8, 256], P(('src', 'tile'), 'gauge'), may hold values from -6 to 6
Outputs:
- theta: float32 [512, 8, 128], P(('src', 'tile'))
- misfit: float32 [128, 4, 8, 256], P(('src', 'tile'), 'gauge')
The draws below stay inside these ranges and needn't reach their ends.
Inputs may be any that keep to these rules, and one draw needn't show every extreme that they name: `footprint`: each source's 2 entries differ. Among the 4 sources of one src and tile index, no value is named more than 2 times, a bound that some block reaches.
All inputs are finite; a program needn't handle non-finite values.
Results may differ from the reference program's by a relative error of at most 0.00017.
Values sent between devices are 32-bit elements; how exact they have to be, the bound alone decides.
A program may use at most 64 MiB of HBM per device.

```python
import math
import jax
import jax.numpy as jnp
import numpy as np
from jax import lax

K = 128
L = 256
FOOT = 2
SRC_DEV = 4
ENS = 8
GN_STEPS = 2
CG_ITERS = 2
SOURCES = 512
TILES = 128
NWIN = 4
CAP = 2
N_SRC = 16
N_TILE = 8


def shard_levels(rng, dims, cuts, least, largest):
    level = 1.0
    for position, shards_of in cuts:
        steps = jax.random.uniform(jax.random.fold_in(jax.random.fold_in(rng, 6), position), (shards_of,), jnp.float32, least / len(cuts), largest / len(cuts))
        level = level * jnp.repeat(jnp.exp(steps), dims[position] // shards_of).reshape((-1,) + (1,) * (len(dims) - 1 - position))
    return level


def assign_block(rng, own, number, rows, number_of, top, limit, lean):
    ranking = jax.random.permutation(rng, number_of)
    packed, common = load_shares(number_of, rows * top, limit, lean, True), load_shares(number_of, rows * top, limit, lean, False)
    places = jnp.arange(number_of)

    def named(lengths, offset_by):
        used = int((lengths > 0).sum())
        fixed = max(1, used // 4)
        shifted = fixed + (places - fixed + offset_by * (used - fixed)) % max(1, number_of - fixed)
        return jnp.zeros((number_of,), jnp.int32).at[ranking[jnp.where(places < fixed, places, shifted)]].set(jnp.asarray(lengths, jnp.int32))

    lengths = jnp.where(number % 4 == 0, named(packed, number // 4), named(common, number - number // 4 - 1))
    mixed = jax.random.permutation(jax.random.fold_in(own, 3), number_of)
    giver, sink = mixed[0:number_of // 2 * 2:2], mixed[1:number_of // 2 * 2:2]
    slack = jnp.minimum(lengths[giver] - 1, limit - lengths[sink]) // 2
    slack = jnp.where((giver == ranking[0]) | (sink == ranking[0]) | (lengths[sink] == 0), 0, jnp.maximum(slack, 0))
    shifted = jax.random.randint(jax.random.fold_in(own, 4), (number_of // 2,), 0, 1 << 20) % (slack + 1)
    lengths = lengths.at[giver].add(-shifted).at[sink].add(shifted)
    items = jnp.searchsorted(jnp.cumsum(lengths), jnp.arange(rows * top), side="right").astype(jnp.int32)
    table = items.reshape(top, rows).T
    table = table[jax.random.permutation(jax.random.fold_in(own, 1), rows)]
    offset_by = jax.random.randint(jax.random.fold_in(own, 2), (rows, 1), 0, top)
    return jnp.take_along_axis(table, (jnp.arange(top)[None, :] + offset_by) % top, axis=1)


def load_shares(amount, total, limit, skew, full):
    portions = [(1 << 20) // math.isqrt(grade ** skew) + 1 for grade in range(1, amount + 1)]
    largest = limit if full else min(limit, max(-(-total // amount), total * portions[0] // sum(portions)))
    least = 1 if total - largest >= amount - 1 else 0
    holding, surplus = [largest] + [least] * (amount - 1), total - largest - least * (amount - 1)
    while surplus > 0:
        movable = [i for i in range(1, amount) if holding[i] < largest] or [i for i in range(1, amount) if holding[i] < limit]
        pool, budget = sum([portions[i] for i in movable]), surplus
        for i in movable:
            extra = min(limit - holding[i], max(1, budget * portions[i] // pool), surplus)
            holding[i] = holding[i] + extra
            surplus = surplus - extra
    return np.array(holding)


def gaussian(own_key, dims, scale, bound, cuts=(), kind=jnp.bfloat16):
    array = jax.random.normal(own_key, dims, jnp.float32) * scale
    if len(cuts) > 0:
        array = shard_levels(own_key, dims, cuts, -0.22, 0.18) * array
    return jnp.clip(array, min=-bound, max=bound).astype(kind)


def setup_inputs(seed: int = 0) -> dict:
    key_of = jax.random.split(jax.random.key(seed), 5)
    responses = gaussian(key_of[0], (SOURCES, FOOT, NWIN, K, L), (K * SRC_DEV * FOOT) ** -0.5, 0.1875, ((0, 128), (2, 4)), jnp.float32)
    footprint_keys = jax.random.split(jax.random.fold_in(key_of[1], 1), SOURCES // SRC_DEV)
    footprint_turns = jax.random.permutation(jax.random.fold_in(key_of[1], 3), SOURCES // SRC_DEV)
    footprint = jax.vmap(lambda own, number: assign_block(jax.random.fold_in(key_of[1], 2), own, number, SRC_DEV, N_SRC, FOOT, CAP, 2))(footprint_keys, footprint_turns).reshape((SOURCES, FOOT))
    theta_start = gaussian(key_of[2], (SOURCES, ENS, K), 1.0, 4.0, ((0, 128),), jnp.float32)
    observed = gaussian(key_of[3], (TILES, NWIN, ENS, L), 1.0, 6.0, ((0, 128), (1, 4)), jnp.float32)
    return {"responses": responses, "footprint": footprint, "theta_start": theta_start, "observed": observed}


damping = 0.1
highest = lax.Precision.HIGHEST


def reference(responses, footprint, theta_start, observed):
    sources = responses.shape[0]
    sector = (jnp.arange(sources, dtype=jnp.int32) // SRC_DEV) % N_TILE
    tile_id = (footprint * N_TILE + sector[:, None]).astype(jnp.int32)
    flat_ids = tile_id.reshape(-1)

    def forward(values):
        terms = jnp.einsum('sek,sfwkl->sfwel', values, responses, precision=highest)
        terms = terms.reshape((-1,) + terms.shape[2:])
        return jax.ops.segment_sum(terms, flat_ids, num_segments=TILES)

    def adjoint(field):
        picked = field[tile_id]
        return jnp.einsum('sfwel,sfwkl->sek', picked, responses, precision=highest)

    theta = theta_start
    misfit = jnp.zeros_like(observed)
    for outer in range(GN_STEPS):
        coef = jax.nn.softplus(theta)
        slope = jax.nn.sigmoid(theta)
        misfit = forward(coef) - observed
        grad = slope * adjoint(misfit) + damping * theta
        update = jnp.zeros_like(theta)
        res = -grad
        direction = res
        norm_now = jnp.sum(res * res, axis=(0, 2))
        for inner in range(CG_ITERS):
            image = forward(slope * direction)
            curv = jnp.sum(image * image, axis=(0, 1, 3)) + damping * jnp.sum(direction * direction, axis=(0, 2))
            alpha = norm_now / curv
            applied = slope * adjoint(image) + damping * direction
            update = update + alpha[None, :, None] * direction
            res = res - alpha[None, :, None] * applied
            norm_next = jnp.sum(res * res, axis=(0, 2))
            direction = res + (norm_next / norm_now)[None, :, None] * direction
            norm_now = norm_next
        theta = theta + update
    return theta, misfit
```

```python
import functools

import jax
import jax.numpy as jnp
from jax import lax
from jax.experimental import pallas as pl
from jax.experimental.pallas import tpu as pltpu
from jax.sharding import PartitionSpec as P

GN_STEPS = 2
DAMPING = 0.1
MESH = pl.DeviceIdType.MESH
F32 = jnp.float32
BF16 = jnp.bfloat16


def split(x):
    hi = x.astype(BF16)
    return hi, (x - hi.astype(F32)).astype(BF16)


def far_first(n):
    return sorted(range(1, n), key=lambda j: (-min(j, n - j), j))


def kernel(
    sizes,
    resp_ref, foot_ref, theta0_ref, obs_ref,
    theta_ref, misfit_ref,
    raw, w,
    terms, arrived, rows_out, rows_in,
    field, gathered_m, gathered_b,
    scal_out, scal_in,
    tile1, tile2,
    adj_g, adj_p, curv_y, last_y,
    load_sem, z_send, z_recv, row_send, row_recv, f_send, f_recv,
    s_send, s_recv, t_send, t_recv, y_send, y_recv, c_send, c_recv,
):
    n_src, n_tile, n_gauge, src_dev, foot = sizes
    blocks = src_dev * foot
    ens, width = theta0_ref.shape[1:]
    length = obs_ref.shape[1]
    me = {"src": lax.axis_index("src"), "tile": lax.axis_index("tile"), "gauge": lax.axis_index("gauge")}
    count = {"src": n_src, "tile": n_tile, "gauge": n_gauge}

    def peers(axis):
        n = count[axis]
        return [lax.rem(me[axis] + j, n) for j in far_first(n)]

    barrier = pltpu.get_barrier_semaphore()
    for axis in ("src", "tile", "gauge"):
        for peer in peers(axis):
            pl.semaphore_signal(barrier, inc=1, device_id={axis: peer}, device_id_type=MESH)

    load = pltpu.make_async_copy(resp_ref, raw, load_sem)
    load.start()
    load.wait()
    for b in range(blocks):
        hi, lo = split(raw[b])
        w[b, 0:width, :] = hi
        w[b, width:2 * width, :] = lo

    pl.semaphore_wait(barrier, n_src + n_tile + n_gauge - 3)

    lanes = lax.broadcasted_iota(jnp.int32, (ens, 128), 1)
    sub = lax.broadcasted_iota(jnp.int32, (ens, 128), 0)

    def to_row(values):
        out = jnp.zeros((ens, 128), F32)
        for i, v in enumerate(values):
            out = out + jnp.where(lanes == sub + i * ens, v, 0.0)
        return jnp.sum(out, axis=0, keepdims=True)

    def from_row(row, i):
        return jnp.sum(jnp.where(lanes == sub + i * ens, row, 0.0), axis=1, keepdims=True)

    def send(axis, src_of, dst, send_sem, recv_sem):
        for peer in peers(axis):
            pltpu.make_async_remote_copy(
                src_ref=src_of(peer), dst_ref=dst.at[me[axis]], send_sem=send_sem, recv_sem=recv_sem,
                device_id={axis: peer}, device_id_type=MESH,
            ).start()

    def drain(ref, sem, n):
        part = ref.at[pl.ds(0, n - 1)]
        pltpu.make_async_copy(part, part, sem).wait()

    def sum_of(ref, n):
        total = ref[0]
        for i in range(1, n):
            total = total + ref[i]
        return total

    def dot_square(a, b):
        return jnp.sum(a * b, axis=tuple(range(a.ndim - 2)) + (a.ndim - 1,)).reshape(ens, 1)

    def forward_terms(x):
        outs = []
        for s in range(src_dev):
            hi, lo = split(x[s])
            left = jnp.concatenate(
                [jnp.concatenate([hi, hi], axis=1), jnp.concatenate([lo, lo], axis=1)], axis=0
            )
            for f in range(foot):
                out = jnp.dot(left, w[s * foot + f], preferred_element_type=F32)
                outs.append(out[0:ens] + out[ens:2 * ens])
        for t in range(n_src):
            total = jnp.zeros((ens, length), F32)
            for b in range(blocks):
                total = total + jnp.where(jnp.full((ens, length), foot_ref[b], jnp.int32) == t, outs[b], 0.0)
            terms[t] = total

    def forward(x, row):
        forward_terms(x)
        send("src", lambda peer: terms.at[peer], arrived, z_send, z_recv)
        if row is not None:
            rows_out[0] = row
            send("src", lambda peer: rows_out.at[0], rows_in, row_send, row_recv)
            rows_in[me["src"]] = row
        arrived[me["src"]] = terms[me["src"]]
        drain(arrived, z_recv, n_src)
        image = sum_of(arrived, n_src)
        row_sum = None
        if row is not None:
            drain(rows_in, row_recv, n_src)
            row_sum = sum_of(rows_in, n_src)
            drain(rows_in, row_send, n_src)
        drain(terms, z_send, n_src)
        return image, row_sum

    def gather(value, dst):
        field[0] = value
        send("src", lambda peer: field.at[0], dst, f_send, f_recv)
        dst[me["src"]] = value
        drain(dst, f_recv, n_src)
        drain(dst, f_send, n_src)

    def adjoint_terms(src, dst):
        mine = me["gauge"]
        for s in range(src_dev):
            total = None
            for f in range(foot):
                b = s * foot + f
                hi, lo = split(src[foot_ref[b]])
                out = lax.dot_general(
                    jnp.concatenate([hi, lo], axis=0), w[b], (((1,), (1,)), ((), ())), preferred_element_type=F32
                )
                out = out[0:ens] + out[ens:2 * ens]
                out = out[:, 0:width] + out[:, width:2 * width]
                total = out if total is None else total + out
            dst[mine, s] = total

    def gauge_sum(dst, i):
        send("gauge", lambda peer: dst.at[me["gauge"]], dst, y_send.at[i], y_recv.at[i])

        def finish():
            drain(dst, y_recv.at[i], n_gauge)
            total = sum_of(dst, n_gauge)
            drain(dst, y_send.at[i], n_gauge)
            return total

        return finish

    def row_exchange(axis, row, out, dst, send_sem, recv_sem):
        out[0] = row
        send(axis, lambda peer: out.at[0], dst, send_sem, recv_sem)
        dst[me[axis]] = row

        def finish():
            drain(dst, recv_sem, count[axis])
            total = sum_of(dst, count[axis])
            drain(dst, send_sem, count[axis])
            return total

        return finish

    theta_ref[...] = theta0_ref[...]

    def step(outer, carry):
        theta = theta_ref[...]
        slope = jax.nn.sigmoid(theta)
        coef = jnp.maximum(theta, 0.0) + jnp.log1p(jnp.exp(-jnp.abs(theta)))

        predicted, _ = forward(coef, None)
        misfit = predicted - obs_ref[...]
        misfit_ref[...] = misfit
        gather(misfit, gathered_m)
        adjoint_terms(gathered_m, adj_g)
        d0 = -(slope * gauge_sum(adj_g, 0)() + DAMPING * theta)

        b0, rr_row = forward(slope * d0, to_row([dot_square(d0, d0)]))
        gather(b0, gathered_b)
        squares = jnp.zeros((ens, length), F32)
        for t in range(n_src):
            squares = squares + gathered_b[t] * gathered_b[t]
        bb = jnp.sum(squares, axis=1, keepdims=True)
        finish_tile = row_exchange(
            "tile", to_row([bb]) + jnp.where(lanes[0:1] < ens, 0.0, pltpu.roll(rr_row, ens, 1)),
            scal_out.at[pl.ds(0, 1)], tile1, t_send.at[0], t_recv.at[0],
        )
        adjoint_terms(gathered_b, adj_p)
        finish_y = gauge_sum(adj_p, 1)
        tile_row = finish_tile()
        finish_c = row_exchange("gauge", tile_row, scal_out.at[pl.ds(1, 1)], curv_y, c_send.at[0], c_recv.at[0])
        p = slope * finish_y() + DAMPING * d0
        bb = from_row(finish_c(), 0)
        rr0 = from_row(tile_row, 1)
        alpha0 = rr0 / (bb + DAMPING * rr0)
        res = d0 - alpha0[None] * p

        image, own_row = forward(slope * res, to_row([dot_square(res, res), dot_square(res, d0)]))
        finish_z = row_exchange(
            "src", to_row([dot_square(image, image), dot_square(image, b0)]),
            scal_out.at[pl.ds(2, 1)], scal_in, s_send, s_recv,
        )
        z_row = finish_z()
        finish_tile = row_exchange(
            "tile", z_row + jnp.where(lanes[0:1] < 2 * ens, 0.0, pltpu.roll(own_row, 2 * ens, 1)),
            scal_out.at[pl.ds(3, 1)], tile2, t_send.at[1], t_recv.at[1],
        )
        tile_row = finish_tile()
        finish_c = row_exchange("gauge", tile_row, scal_out.at[pl.ds(4, 1)], last_y, c_send.at[1], c_recv.at[1])
        all_row = finish_c()
        cc, cb = from_row(all_row, 0), from_row(all_row, 1)
        rr1, rd = from_row(tile_row, 2), from_row(tile_row, 3)
        beta = rr1 / rr0
        curv = cc + beta * (2.0 * cb + beta * bb) + DAMPING * (rr1 + beta * (2.0 * rd + beta * rr0))
        alpha1 = rr1 / curv
        update = alpha0[None] * d0 + alpha1[None] * (res + beta[None] * d0)
        theta_ref[...] = theta + update
        return carry

    lax.fori_loop(0, GN_STEPS, step, 0)


def local(sizes, responses, footprint, theta_start, observed):
    n_src, n_tile, n_gauge = sizes
    src_dev, foot, _, width, length = responses.shape
    ens = theta_start.shape[1]
    blocks = src_dev * foot
    vmem = pl.BlockSpec(memory_space=pltpu.VMEM)
    dma = pltpu.SemaphoreType.DMA
    row = (1, 128)
    theta, misfit = pl.pallas_call(
        functools.partial(kernel, (n_src, n_tile, n_gauge, src_dev, foot)),
        out_shape=(
            jax.ShapeDtypeStruct(theta_start.shape, F32),
            jax.ShapeDtypeStruct((ens, length), F32),
        ),
        in_specs=[pl.BlockSpec(memory_space=pl.ANY), pl.BlockSpec(memory_space=pltpu.SMEM), vmem, vmem],
        out_specs=(vmem, vmem),
        scratch_shapes=[
            pltpu.VMEM((blocks, width, length), F32),
            pltpu.VMEM((blocks, 2 * width, length), BF16),
            pltpu.VMEM((n_src, ens, length), F32),
            pltpu.VMEM((n_src, ens, length), F32),
            pltpu.VMEM((1,) + row, F32),
            pltpu.VMEM((n_src,) + row, F32),
            pltpu.VMEM((1, ens, length), F32),
            pltpu.VMEM((n_src, ens, length), F32),
            pltpu.VMEM((n_src, ens, length), F32),
            pltpu.VMEM((5,) + row, F32),
            pltpu.VMEM((n_src,) + row, F32),
            pltpu.VMEM((n_tile,) + row, F32),
            pltpu.VMEM((n_tile,) + row, F32),
            pltpu.VMEM((n_gauge, src_dev, ens, width), F32),
            pltpu.VMEM((n_gauge, src_dev, ens, width), F32),
            pltpu.VMEM((n_gauge,) + row, F32),
            pltpu.VMEM((n_gauge,) + row, F32),
            dma, dma, dma, dma, dma, dma, dma,
            dma, dma, dma((2,)), dma((2,)), dma((2,)), dma((2,)), dma((2,)), dma((2,)),
        ],
        compiler_params=pltpu.CompilerParams(collective_id=0, has_side_effects=True),
    )(
        responses.reshape(blocks, width, length),
        footprint.reshape(blocks),
        theta_start,
        observed.reshape(ens, length),
    )
    return theta, misfit.reshape(observed.shape)


def solution(mesh):
    sizes = (mesh.shape["src"], mesh.shape["tile"], mesh.shape["gauge"])
    in_specs = (
        P(("src", "tile"), None, "gauge", None, None),
        P(("src", "tile"), None),
        P(("src", "tile"), None, None),
        P(("src", "tile"), "gauge", None, None),
    )
    out_specs = (P(("src", "tile"), None, None), P(("src", "tile"), "gauge", None, None))
    return jax.shard_map(
        functools.partial(local, sizes), mesh=mesh, in_specs=in_specs, out_specs=out_specs, check_vma=False
    )
```

```python
import functools

import jax
import jax.numpy as jnp
from jax import lax
from jax.experimental import pallas as pl
from jax.experimental.pallas import tpu as pltpu
from jax.sharding import PartitionSpec as P

GN_STEPS = 2
DAMPING = 0.1
MESH = pl.DeviceIdType.MESH
F32 = jnp.float32
BF16 = jnp.bfloat16


def split(x):
    hi = x.astype(BF16)
    return hi, (x - hi.astype(F32)).astype(BF16)


def far_first(n):
    return sorted(range(1, n), key=lambda j: (-min(j, n - j), j))


def kernel(
    sizes,
    resp_hbm, foot_hbm, theta_hbm, obs_hbm,
    theta_ref, misfit_ref,
    raw, w, foot_ref, theta0, obs,
    terms, arrived, rows_out, rows_in,
    field, gathered_m, gathered_b,
    adj_g, adj_p, scal_in, plane_a, plane_b,
    load_sem, z_send, z_recv, f_send, f_recv, y_send, y_recv, r_send, r_recv, p_send, p_recv,
):
    n_src, n_tile, n_gauge, src_dev, foot = sizes
    blocks = src_dev * foot
    ens, width = theta0.shape[1:]
    length = obs.shape[1]
    my_src, my_tile, my_gauge = lax.axis_index("src"), lax.axis_index("tile"), lax.axis_index("gauge")

    src_peers = [lax.rem(my_src + j, n_src) for j in far_first(n_src)]
    gauge_peers = [lax.rem(my_gauge + j, n_gauge) for j in far_first(n_gauge)]

    def hops(ab):
        a, b = ab[0] // 2, ab[1]
        return -(min(a, n_tile // 2 - a) + min(b, n_gauge - b))

    plane_peers = [
        {"tile": lax.rem(my_tile + a, n_tile), "gauge": lax.rem(my_gauge + b, n_gauge)}
        for a, b in sorted([(a, b) for a in range(n_tile) for b in range(n_gauge) if a or b], key=hops)
    ]
    my_plane = my_tile * n_gauge + my_gauge
    n_plane = n_tile * n_gauge

    barrier = pltpu.get_barrier_semaphore()
    for peer in [{"src": p} for p in src_peers] + plane_peers:
        pl.semaphore_signal(barrier, inc=1, device_id=peer, device_id_type=MESH)

    loads = [
        pltpu.make_async_copy(a, b, load_sem.at[i])
        for i, (a, b) in enumerate(
            [(theta_hbm, theta0), (resp_hbm, raw), (foot_hbm, foot_ref), (obs_hbm, obs)]
        )
    ]
    for load in loads:
        load.start()

    lanes = lax.broadcasted_iota(jnp.int32, (ens, 128), 1)
    sub = lax.broadcasted_iota(jnp.int32, (ens, 128), 0)

    def to_row(values):
        out = jnp.zeros((ens, 128), F32)
        for i, v in enumerate(values):
            out = out + jnp.where(lanes == sub + i * ens, v, 0.0)
        return jnp.sum(out, axis=0, keepdims=True)

    def from_row(row, i):
        return jnp.sum(jnp.where(lanes == sub + i * ens, row, 0.0), axis=1, keepdims=True)

    def copy(src, dst, send_sem, recv_sem, peer):
        pltpu.make_async_remote_copy(
            src_ref=src, dst_ref=dst, send_sem=send_sem, recv_sem=recv_sem,
            device_id=peer, device_id_type=MESH,
        ).start()

    def drain(ref, sem, n):
        part = ref.at[pl.ds(0, n - 1)]
        pltpu.make_async_copy(part, part, sem).wait()

    def sum_of(ref, n):
        parts = [ref[i] for i in range(n)]
        while len(parts) > 1:
            parts = [sum(parts[i:i + 2]) for i in range(0, len(parts), 2)]
        return parts[0]

    def inner(a, b):
        prod = a * b
        if prod.ndim == 3:
            prod = sum(prod[i] for i in range(prod.shape[0]))
        return jnp.sum(prod, axis=1, keepdims=True)

    def forward_terms(x):
        outs = []
        for s in range(src_dev):
            hi, lo = split(x[s])
            left = jnp.concatenate(
                [jnp.concatenate([hi, hi], axis=1), jnp.concatenate([lo, lo], axis=1)], axis=0
            )
            for f in range(foot):
                out = jnp.dot(left, w[s * foot + f], preferred_element_type=F32)
                outs.append(out[0:ens] + out[ens:2 * ens])
        for t in range(n_src):
            total = jnp.zeros((ens, length), F32)
            for b in range(blocks):
                mine = jnp.full((ens, length), foot_ref[b % foot, b // foot], jnp.int32) == t
                total = total + jnp.where(mine, outs[b], 0.0)
            terms[t] = total

    def scatter_start():
        for peer in src_peers:
            copy(terms.at[peer], arrived.at[my_src], z_send, z_recv, {"src": peer})
        arrived[my_src] = terms[my_src]

    def scatter_finish():
        drain(arrived, z_recv, n_src)
        return sum_of(arrived, n_src)

    def gather_start(value, dst):
        field[0] = value
        for peer in src_peers:
            copy(field.at[0], dst.at[my_src], f_send, f_recv, {"src": peer})
        dst[my_src] = value

    def adjoint_terms(src, dst):
        for s in range(src_dev):
            total = None
            for f in range(foot):
                hi, lo = split(src[foot_ref[f, s]])
                out = lax.dot_general(
                    jnp.concatenate([hi, lo], axis=0), w[s * foot + f],
                    (((1,), (1,)), ((), ())), preferred_element_type=F32,
                )
                out = out[0:ens] + out[ens:2 * ens]
                out = out[:, 0:width] + out[:, width:2 * width]
                total = out if total is None else total + out
            dst[my_gauge, s] = total

    def gauge_start(dst, i):
        for peer in gauge_peers:
            copy(dst.at[my_gauge], dst.at[my_gauge], y_send.at[i], y_recv.at[i], {"gauge": peer})

    def gauge_finish(dst, i):
        drain(dst, y_recv.at[i], n_gauge)
        return sum_of(dst, n_gauge)

    def rows_start(row, dst, i):
        rows_out[i] = row
        for peer in src_peers:
            copy(rows_out.at[i], dst.at[my_src], r_send.at[i], r_recv.at[i], {"src": peer})
        dst[my_src] = row

    def rows_finish(dst, i):
        drain(dst, r_recv.at[i], n_src)
        return sum_of(dst, n_src)

    def plane_start(row, dst, i):
        rows_out[2 + i] = row
        for peer in plane_peers:
            copy(rows_out.at[2 + i], dst.at[my_plane], p_send.at[i], p_recv.at[i], peer)
        dst[my_plane] = row

    def plane_finish(dst, i):
        drain(dst, p_recv.at[i], n_plane)
        return sum_of(dst, n_plane)

    for i in (0, 1, 2):
        loads[i].wait()
    for b in range(blocks):
        hi, lo = split(raw[b])
        w[b, 0:width, :] = hi
        w[b, width:2 * width, :] = lo
    theta = theta0[...]

    for outer in range(GN_STEPS):
        slope = jax.nn.sigmoid(theta)
        coef = jnp.maximum(theta, 0.0) + jnp.log1p(jnp.exp(-jnp.abs(theta)))

        forward_terms(coef)
        if outer == 0:
            pl.semaphore_wait(barrier, n_src + n_plane - 2)
        scatter_start()
        if outer == 0:
            loads[3].wait()
        misfit = scatter_finish() - obs[...]
        gather_start(misfit, gathered_m)
        if outer + 1 == GN_STEPS:
            misfit_ref[...] = misfit
        drain(terms, z_send, n_src)
        drain(gathered_m, f_recv, n_src)
        adjoint_terms(gathered_m, adj_g)
        gauge_start(adj_g, 0)
        drain(gathered_m, f_send, n_src)
        d0 = -(slope * gauge_finish(adj_g, 0) + DAMPING * theta)

        forward_terms(slope * d0)
        scatter_start()
        rows_start(to_row([inner(d0, d0)]), rows_in, 0)
        drain(adj_g, y_send.at[0], n_gauge)
        b0 = scatter_finish()
        gather_start(b0, gathered_b)
        drain(terms, z_send, n_src)
        rr_row = rows_finish(rows_in, 0)
        drain(rows_in, r_send.at[0], n_src)
        drain(gathered_b, f_recv, n_src)
        adjoint_terms(gathered_b, adj_p)
        gauge_start(adj_p, 1)
        squares = gathered_b[0] * gathered_b[0]
        for t in range(1, n_src):
            squares = squares + gathered_b[t] * gathered_b[t]
        bb_row = to_row([jnp.sum(squares, axis=1, keepdims=True)])
        plane_start(bb_row + jnp.where(lanes[0:1] < ens, 0.0, pltpu.roll(rr_row, ens, 1)), plane_a, 0)
        drain(gathered_b, f_send, n_src)
        p = slope * gauge_finish(adj_p, 1) + DAMPING * d0

        forward_terms(slope * p)
        scatter_start()
        drain(adj_p, y_send.at[1], n_gauge)
        row = plane_finish(plane_a, 0)
        bb, rr0 = from_row(row, 0), from_row(row, 1) * (1.0 / n_gauge)
        alpha0 = rr0 / (bb + DAMPING * rr0)
        res = d0 - alpha0[None] * p
        rr1, rd = inner(res, res), inner(res, d0)
        drain(plane_a, p_send.at[0], n_plane)
        image = b0 - alpha0 * scatter_finish()
        rows_start(to_row([inner(image, image), inner(image, b0), rr1, rd]), scal_in, 1)
        drain(terms, z_send, n_src)
        plane_start(rows_finish(scal_in, 1), plane_b, 1)
        drain(scal_in, r_send.at[1], n_src)
        row = plane_finish(plane_b, 1)
        cc, cb = from_row(row, 0), from_row(row, 1)
        rr1, rd = from_row(row, 2) * (1.0 / n_gauge), from_row(row, 3) * (1.0 / n_gauge)
        beta = rr1 / rr0
        curv = cc + beta * (2.0 * cb + beta * bb) + DAMPING * (rr1 + beta * (2.0 * rd + beta * rr0))
        alpha1 = rr1 / curv
        theta = theta + (alpha0[None] * d0 + alpha1[None] * (res + beta[None] * d0))
        drain(plane_b, p_send.at[1], n_plane)
    theta_ref[...] = theta


def local(sizes, responses, footprint, theta_start, observed):
    n_src, n_tile, n_gauge = sizes
    src_dev, foot, _, width, length = responses.shape
    ens = theta_start.shape[1]
    blocks = src_dev * foot
    vmem, anywhere = pl.BlockSpec(memory_space=pltpu.VMEM), pl.BlockSpec(memory_space=pl.ANY)
    dma = pltpu.SemaphoreType.DMA
    row = (1, 128)
    theta, misfit = pl.pallas_call(
        functools.partial(kernel, (n_src, n_tile, n_gauge, src_dev, foot)),
        out_shape=(
            jax.ShapeDtypeStruct(theta_start.shape, F32),
            jax.ShapeDtypeStruct((ens, length), F32),
        ),
        in_specs=[anywhere] * 4,
        out_specs=(vmem, vmem),
        scratch_shapes=[
            pltpu.VMEM((blocks, width, length), F32),
            pltpu.VMEM((blocks, 2 * width, length), BF16),
            pltpu.SMEM((foot, src_dev), jnp.int32),
            pltpu.VMEM((src_dev, ens, width), F32),
            pltpu.VMEM((ens, length), F32),
            pltpu.VMEM((n_src, ens, length), F32),
            pltpu.VMEM((n_src, ens, length), F32),
            pltpu.VMEM((4,) + row, F32),
            pltpu.VMEM((n_src,) + row, F32),
            pltpu.VMEM((1, ens, length), F32),
            pltpu.VMEM((n_src, ens, length), F32),
            pltpu.VMEM((n_src, ens, length), F32),
            pltpu.VMEM((n_gauge, src_dev, ens, width), F32),
            pltpu.VMEM((n_gauge, src_dev, ens, width), F32),
            pltpu.VMEM((n_src,) + row, F32),
            pltpu.VMEM((n_tile * n_gauge,) + row, F32),
            pltpu.VMEM((n_tile * n_gauge,) + row, F32),
            dma((4,)), dma, dma, dma, dma,
            dma((2,)), dma((2,)), dma((2,)), dma((2,)), dma((2,)), dma((2,)),
        ],
        compiler_params=pltpu.CompilerParams(collective_id=0, has_side_effects=True),
    )(
        responses.reshape(blocks, width, length),
        footprint.T,
        theta_start,
        observed.reshape(ens, length),
    )
    return theta, misfit.reshape(observed.shape)


def solution(mesh):
    sizes = (mesh.shape["src"], mesh.shape["tile"], mesh.shape["gauge"])
    in_specs = (
        P(("src", "tile"), None, "gauge", None, None),
        P(("src", "tile"), None),
        P(("src", "tile"), None, None),
        P(("src", "tile"), "gauge", None, None),
    )
    out_specs = (P(("src", "tile"), None, None), P(("src", "tile"), "gauge", None, None))
    return jax.shard_map(
        functools.partial(local, sizes), mesh=mesh, in_specs=in_specs, out_specs=out_specs, check_vma=False
    )
```

```python
import functools

import jax
import jax.numpy as jnp
from jax import lax
from jax.experimental import pallas as pl
from jax.experimental.pallas import tpu as pltpu
from jax.sharding import PartitionSpec as P

GN_STEPS = 2
DAMPING = 0.1
MESH = pl.DeviceIdType.MESH
F32 = jnp.float32
BF16 = jnp.bfloat16


def split(x):
    hi = x.astype(BF16)
    return hi, (x - hi.astype(F32)).astype(BF16)


def far_first(n):
    return sorted(range(1, n), key=lambda j: (-min(j, n - j), j))


def kernel(
    sizes,
    resp_hbm, foot_hbm, theta_hbm, obs_hbm,
    theta_ref, misfit_ref,
    raw, w, foot_ref, theta0, obs,
    terms, arrived, rows_out, rows_in,
    field, gathered_m, gathered_b,
    adj_g, adj_p, scal_in, plane_a, plane_b, relayed, joined,
    load_sem, relay_send, relay_recv, z_send, z_recv, f_send, f_recv, y_send, y_recv, r_send, r_recv, p_send, p_recv,
):
    n_src, n_tile, n_gauge, src_dev, foot = sizes
    blocks = src_dev * foot
    ens, width = theta0.shape[1:]
    length = obs.shape[1]
    my_src, my_tile, my_gauge = lax.axis_index("src"), lax.axis_index("tile"), lax.axis_index("gauge")

    turn = 1 - 2 * lax.rem(my_tile, 2)

    def at(j):
        return lax.rem(my_src + n_src + turn * j, n_src)

    near = n_src // 4
    near_js = [sign * j for j in range(near, 0, -1) for sign in (1, -1)]
    src_peers = [at(j) for j in far_first(n_src)]
    gauge_peers = [lax.rem(my_gauge + j, n_gauge) for j in far_first(n_gauge)]

    def hops(ab):
        a, b = ab[0] // 2, ab[1]
        return -(min(a, n_tile // 2 - a) + min(b, n_gauge - b))

    plane_peers = [
        {"tile": lax.rem(my_tile + a, n_tile), "gauge": lax.rem(my_gauge + b, n_gauge)}
        for a, b in sorted([(a, b) for a in range(n_tile) for b in range(n_gauge) if a or b], key=hops)
    ]
    my_plane = my_tile * n_gauge + my_gauge
    n_plane = n_tile * n_gauge

    barrier = pltpu.get_barrier_semaphore()
    for peer in [{"src": at(j)} for j in near_js] + plane_peers:
        pl.semaphore_signal(barrier, inc=1, device_id=peer, device_id_type=MESH)

    loads = [
        pltpu.make_async_copy(a, b, load_sem.at[i])
        for i, (a, b) in enumerate(
            [(theta_hbm, theta0), (resp_hbm, raw), (foot_hbm, foot_ref), (obs_hbm, obs)]
        )
    ]
    for load in loads:
        load.start()

    lanes = lax.broadcasted_iota(jnp.int32, (ens, 128), 1)
    sub = lax.broadcasted_iota(jnp.int32, (ens, 128), 0)

    def to_row(values):
        out = jnp.zeros((ens, 128), F32)
        for i, v in enumerate(values):
            out = out + jnp.where(lanes == sub + i * ens, v, 0.0)
        return jnp.sum(out, axis=0, keepdims=True)

    def from_row(row, i):
        return jnp.sum(jnp.where(lanes == sub + i * ens, row, 0.0), axis=1, keepdims=True)

    def copy(src, dst, send_sem, recv_sem, peer):
        pltpu.make_async_remote_copy(
            src_ref=src, dst_ref=dst, send_sem=send_sem, recv_sem=recv_sem,
            device_id=peer, device_id_type=MESH,
        ).start()

    def drain(ref, sem, n):
        part = ref.at[pl.ds(0, n - 1)]
        pltpu.make_async_copy(part, part, sem).wait()

    def sum_of(ref, n):
        parts = [ref[i] for i in range(n)]
        while len(parts) > 1:
            parts = [sum(parts[i:i + 2]) for i in range(0, len(parts), 2)]
        return parts[0]

    def inner(a, b):
        prod = a * b
        if prod.ndim == 3:
            prod = sum(prod[i] for i in range(prod.shape[0]))
        return jnp.sum(prod, axis=1, keepdims=True)

    def forward_terms(x):
        outs = []
        for s in range(src_dev):
            hi, lo = split(x[s])
            left = jnp.concatenate(
                [jnp.concatenate([hi, hi], axis=1), jnp.concatenate([lo, lo], axis=1)], axis=0
            )
            for f in range(foot):
                out = jnp.dot(left, w[s * foot + f], preferred_element_type=F32)
                outs.append(out[0:ens] + out[ens:2 * ens])
        for t in range(n_src):
            total = jnp.zeros((ens, length), F32)
            for b in range(blocks):
                mine = jnp.full((ens, length), foot_ref[b % foot, b // foot], jnp.int32) == t
                total = total + jnp.where(mine, outs[b], 0.0)
            terms[t] = total

    def first_scatter():
        for j in range(2 * near, near, -1):
            copy(terms.at[at(j)], relayed.at[j - near - 1], relay_send, relay_recv.at[0], {"src": at(near)})
            if j < 2 * near:
                copy(terms.at[at(-j)], relayed.at[j - 1], relay_send, relay_recv.at[1], {"src": at(-near)})
        copy(terms.at[at(-near)], arrived.at[my_src], z_send, z_recv, {"src": at(-near)})
        for side, sign, first, n in ((0, 1, 0, near), (1, -1, near, near - 1)):
            if n == 0:
                continue
            part = relayed.at[pl.ds(first, n)]
            pltpu.make_async_copy(part, part, relay_recv.at[side]).wait()
            for j in range(n, 0, -1):
                slot = first + j - 1
                joined[slot] = relayed[slot] + terms[at(sign * j)]
                copy(joined.at[slot], arrived.at[my_src], z_send, z_recv, {"src": at(sign * j)})
        total = terms[my_src]
        drain(arrived, z_recv, 2 * near + 1)
        for j in near_js:
            total = total + arrived[at(j)]
        drain(arrived, z_send, 2 * near + 1)
        drain(relayed, relay_send, 2 * near)
        return total

    def scatter_start():
        for peer in src_peers:
            copy(terms.at[peer], arrived.at[my_src], z_send, z_recv, {"src": peer})
        arrived[my_src] = terms[my_src]

    def scatter_finish():
        drain(arrived, z_recv, n_src)
        return sum_of(arrived, n_src)

    def gather_start(value, dst):
        field[0] = value
        for peer in src_peers:
            copy(field.at[0], dst.at[my_src], f_send, f_recv, {"src": peer})
        dst[my_src] = value

    def adjoint_terms(src, dst):
        for s in range(src_dev):
            total = None
            for f in range(foot):
                hi, lo = split(src[foot_ref[f, s]])
                out = lax.dot_general(
                    jnp.concatenate([hi, lo], axis=0), w[s * foot + f],
                    (((1,), (1,)), ((), ())), preferred_element_type=F32,
                )
                out = out[0:ens] + out[ens:2 * ens]
                out = out[:, 0:width] + out[:, width:2 * width]
                total = out if total is None else total + out
            dst[my_gauge, s] = total

    def gauge_start(dst, i):
        for peer in gauge_peers:
            copy(dst.at[my_gauge], dst.at[my_gauge], y_send.at[i], y_recv.at[i], {"gauge": peer})

    def gauge_finish(dst, i):
        drain(dst, y_recv.at[i], n_gauge)
        return sum_of(dst, n_gauge)

    def rows_start(row, dst, i):
        rows_out[i] = row
        for peer in src_peers:
            copy(rows_out.at[i], dst.at[my_src], r_send.at[i], r_recv.at[i], {"src": peer})
        dst[my_src] = row

    def rows_finish(dst, i):
        drain(dst, r_recv.at[i], n_src)
        return sum_of(dst, n_src)

    def plane_start(row, dst, i):
        rows_out[2 + i] = row
        for peer in plane_peers:
            copy(rows_out.at[2 + i], dst.at[my_plane], p_send.at[i], p_recv.at[i], peer)
        dst[my_plane] = row

    def plane_finish(dst, i):
        drain(dst, p_recv.at[i], n_plane)
        return sum_of(dst, n_plane)

    for i in (0, 1, 2):
        loads[i].wait()
    for b in range(blocks):
        hi, lo = split(raw[b])
        w[b, 0:width, :] = hi
        w[b, width:2 * width, :] = lo
    theta = theta0[...]

    for outer in range(GN_STEPS):
        slope = jax.nn.sigmoid(theta)
        coef = jnp.maximum(theta, 0.0) + jnp.log1p(jnp.exp(-jnp.abs(theta)))

        forward_terms(coef)
        if outer == 0:
            pl.semaphore_wait(barrier, 2 * near + n_plane - 1)
            loads[3].wait()
            misfit = first_scatter() - obs[...]
        else:
            scatter_start()
            misfit = scatter_finish() - obs[...]
        gather_start(misfit, gathered_m)
        if outer + 1 == GN_STEPS:
            misfit_ref[...] = misfit
        if outer > 0:
            drain(terms, z_send, n_src)
        drain(gathered_m, f_recv, n_src)
        adjoint_terms(gathered_m, adj_g)
        gauge_start(adj_g, 0)
        drain(gathered_m, f_send, n_src)
        d0 = -(slope * gauge_finish(adj_g, 0) + DAMPING * theta)

        forward_terms(slope * d0)
        scatter_start()
        rows_start(to_row([inner(d0, d0)]), rows_in, 0)
        drain(adj_g, y_send.at[0], n_gauge)
        b0 = scatter_finish()
        gather_start(b0, gathered_b)
        drain(terms, z_send, n_src)
        rr_row = rows_finish(rows_in, 0)
        drain(rows_in, r_send.at[0], n_src)
        drain(gathered_b, f_recv, n_src)
        adjoint_terms(gathered_b, adj_p)
        gauge_start(adj_p, 1)
        squares = gathered_b[0] * gathered_b[0]
        for t in range(1, n_src):
            squares = squares + gathered_b[t] * gathered_b[t]
        bb_row = to_row([jnp.sum(squares, axis=1, keepdims=True)])
        plane_start(bb_row + jnp.where(lanes[0:1] < ens, 0.0, pltpu.roll(rr_row, ens, 1)), plane_a, 0)
        drain(gathered_b, f_send, n_src)
        p = slope * gauge_finish(adj_p, 1) + DAMPING * d0

        forward_terms(slope * p)
        scatter_start()
        drain(adj_p, y_send.at[1], n_gauge)
        row = plane_finish(plane_a, 0)
        bb, rr0 = from_row(row, 0), from_row(row, 1) * (1.0 / n_gauge)
        alpha0 = rr0 / (bb + DAMPING * rr0)
        res = d0 - alpha0[None] * p
        rr1, rd = inner(res, res), inner(res, d0)
        drain(plane_a, p_send.at[0], n_plane)
        image = b0 - alpha0 * scatter_finish()
        rows_start(to_row([inner(image, image), inner(image, b0), rr1, rd]), scal_in, 1)
        drain(terms, z_send, n_src)
        plane_start(rows_finish(scal_in, 1), plane_b, 1)
        drain(scal_in, r_send.at[1], n_src)
        row = plane_finish(plane_b, 1)
        cc, cb = from_row(row, 0), from_row(row, 1)
        rr1, rd = from_row(row, 2) * (1.0 / n_gauge), from_row(row, 3) * (1.0 / n_gauge)
        beta = rr1 / rr0
        curv = cc + beta * (2.0 * cb + beta * bb) + DAMPING * (rr1 + beta * (2.0 * rd + beta * rr0))
        alpha1 = rr1 / curv
        theta = theta + (alpha0[None] * d0 + alpha1[None] * (res + beta[None] * d0))
        drain(plane_b, p_send.at[1], n_plane)
    theta_ref[...] = theta


def hand_over(theta_in, misfit_in, theta_out, misfit_out):
    theta_out[...] = theta_in[...]
    misfit_out[...] = misfit_in[...]


def local(sizes, responses, footprint, theta_start, observed):
    n_src, n_tile, n_gauge = sizes
    src_dev, foot, _, width, length = responses.shape
    ens = theta_start.shape[1]
    blocks = src_dev * foot
    vmem, anywhere = pl.BlockSpec(memory_space=pltpu.VMEM), pl.BlockSpec(memory_space=pl.ANY)
    dma = pltpu.SemaphoreType.DMA
    row = (1, 128)
    theta, misfit = pl.pallas_call(
        functools.partial(kernel, (n_src, n_tile, n_gauge, src_dev, foot)),
        out_shape=(
            jax.ShapeDtypeStruct(theta_start.shape, F32),
            jax.ShapeDtypeStruct((ens, length), F32),
        ),
        in_specs=[anywhere] * 4,
        out_specs=(vmem, vmem),
        scratch_shapes=[
            pltpu.VMEM((blocks, width, length), F32),
            pltpu.VMEM((blocks, 2 * width, length), BF16),
            pltpu.SMEM((foot, src_dev), jnp.int32),
            pltpu.VMEM((src_dev, ens, width), F32),
            pltpu.VMEM((ens, length), F32),
            pltpu.VMEM((n_src, ens, length), F32),
            pltpu.VMEM((n_src, ens, length), F32),
            pltpu.VMEM((4,) + row, F32),
            pltpu.VMEM((n_src,) + row, F32),
            pltpu.VMEM((1, ens, length), F32),
            pltpu.VMEM((n_src, ens, length), F32),
            pltpu.VMEM((n_src, ens, length), F32),
            pltpu.VMEM((n_gauge, src_dev, ens, width), F32),
            pltpu.VMEM((n_gauge, src_dev, ens, width), F32),
            pltpu.VMEM((n_src,) + row, F32),
            pltpu.VMEM((n_tile * n_gauge,) + row, F32),
            pltpu.VMEM((n_tile * n_gauge,) + row, F32),
            pltpu.VMEM((n_src // 2, ens, length), F32),
            pltpu.VMEM((n_src // 2, ens, length), F32),
            dma((4,)), dma, dma((2,)), dma, dma, dma, dma,
            dma((2,)), dma((2,)), dma((2,)), dma((2,)), dma((2,)), dma((2,)),
        ],
        compiler_params=pltpu.CompilerParams(collective_id=0, has_side_effects=True),
    )(
        responses.reshape(blocks, width, length),
        footprint.T,
        theta_start,
        observed.reshape(ens, length),
    )
    theta, misfit = pl.pallas_call(
        hand_over,
        out_shape=(
            jax.ShapeDtypeStruct(theta_start.shape, F32),
            jax.ShapeDtypeStruct((ens, length), F32),
        ),
        in_specs=[vmem, vmem],
        out_specs=(vmem, vmem),
    )(theta, misfit)
    return theta, misfit.reshape(observed.shape)


def solution(mesh):
    sizes = (mesh.shape["src"], mesh.shape["tile"], mesh.shape["gauge"])
    in_specs = (
        P(("src", "tile"), None, "gauge", None, None),
        P(("src", "tile"), None),
        P(("src", "tile"), None, None),
        P(("src", "tile"), "gauge", None, None),
    )
    out_specs = (P(("src", "tile"), None, None), P(("src", "tile"), "gauge", None, None))
    return jax.shard_map(
        functools.partial(local, sizes), mesh=mesh, in_specs=in_specs, out_specs=out_specs, check_vma=False
    )
```

```python
import functools

import jax
import jax.numpy as jnp
from jax import lax
from jax.experimental import pallas as pl
from jax.experimental.pallas import tpu as pltpu
from jax.sharding import PartitionSpec as P

GN_STEPS = 2
DAMPING = 0.1
MESH = pl.DeviceIdType.MESH
F32 = jnp.float32
BF16 = jnp.bfloat16


def split(x):
    hi = x.astype(BF16)
    return hi, (x - hi.astype(F32)).astype(BF16)


def far_first(n):
    return sorted(range(1, n), key=lambda j: (-min(j, n - j), j))


def kernel(
    sizes,
    resp_hbm, foot_hbm, theta_hbm, obs_hbm,
    theta_ref, misfit_ref,
    raw, w, foot_ref, theta0, obs, load_sem, *scratch,
):
    n_src, n_tile, n_gauge, src_dev, foot = sizes
    blocks = src_dev * foot
    ens, width = theta0.shape[1:]
    half, lane_half = ens // 2, obs.shape[1] // 2
    my_src, my_tile, my_gauge = lax.axis_index("src"), lax.axis_index("tile"), lax.axis_index("gauge")

    src_peers = [lax.rem(my_src + j, n_src) for j in far_first(n_src)]
    gauge_peers = [lax.rem(my_gauge + j, n_gauge) for j in far_first(n_gauge)]

    def hops(ab):
        a, b = ab[0] // 2, ab[1]
        return -(min(a, n_tile // 2 - a) + min(b, n_gauge - b))

    plane_peers = [
        {"tile": lax.rem(my_tile + a, n_tile), "gauge": lax.rem(my_gauge + b, n_gauge)}
        for a, b in sorted([(a, b) for a in range(n_tile) for b in range(n_gauge) if a or b], key=hops)
    ]
    my_plane = my_tile * n_gauge + my_gauge
    n_plane = n_tile * n_gauge

    loads = [
        pltpu.make_async_copy(a, b, load_sem.at[i])
        for i, (a, b) in enumerate(
            [(theta_hbm, theta0), (foot_hbm, foot_ref)]
            + [(resp_hbm.at[pl.ds(s * foot, foot)], raw.at[pl.ds(s * foot, foot)]) for s in range(src_dev)]
            + [(obs_hbm, obs)]
        )
    ]
    for load in loads:
        load.start()

    barrier = pltpu.get_barrier_semaphore()
    for peer in [{"src": p} for p in src_peers] + plane_peers:
        pl.semaphore_signal(barrier, inc=1, device_id=peer, device_id_type=MESH)

    lanes = lax.broadcasted_iota(jnp.int32, (ens, 128), 1)
    sub = lax.broadcasted_iota(jnp.int32, (ens, 128), 0)
    upper = sub < half
    place = jnp.where(upper, sub, sub - half)

    def swap(x):
        return pltpu.roll(x, half, 0)

    def to_row(values):
        out = jnp.zeros((ens, 128), F32)
        for i, v in enumerate(values):
            out = out + jnp.where(lanes == place + i * half, v, 0.0)
        return jnp.sum(out, axis=0, keepdims=True)

    def from_row(row, i):
        return jnp.sum(jnp.where(lanes == place + i * half, row, 0.0), axis=1, keepdims=True)

    def copy(src, dst, send_sem, recv_sem, peer):
        pltpu.make_async_remote_copy(
            src_ref=src, dst_ref=dst, send_sem=send_sem, recv_sem=recv_sem,
            device_id=peer, device_id_type=MESH,
        ).start()

    def drain(ref, sem, n):
        part = ref.at[pl.ds(0, n - 1)]
        pltpu.make_async_copy(part, part, sem).wait()

    def tree(parts):
        while len(parts) > 1:
            parts = [sum(parts[i:i + 2]) for i in range(0, len(parts), 2)]
        return parts[0]

    def sum_of(ref, n):
        return tree([ref[i] for i in range(n)])

    def inner(a, b):
        return 0.5 * jnp.sum(tree([a[s] * b[s] for s in range(src_dev)]), axis=1, keepdims=True)

    def inner_tile(a, b):
        return jnp.sum(a * b, axis=1, keepdims=True)

    def products(x):
        outs = []
        for s in range(src_dev):
            hi, lo = split(x[s])
            left = jnp.concatenate(
                [jnp.concatenate([hi, hi], axis=1), jnp.concatenate([lo, lo], axis=1)], axis=0
            )
            for f in range(foot):
                out = jnp.dot(left, w[s * foot + f], preferred_element_type=F32)
                out = out[0:ens] + out[ens:2 * ens]
                outs.append(jnp.where(upper, out[:, 0:lane_half], out[:, lane_half:]))
        return outs

    results = {}

    def chain(h, refs):
        (
            terms, arrived, field, gathered_m, gathered_b, adj_g, adj_p,
            rows_out, rows_in, scal_in, plane_a, plane_b,
            z_send, z_recv, f_send, f_recv, y_send, y_recv, r_send, r_recv, p_send, p_recv,
        ) = refs

        def scatter_start(outs):
            names = [jnp.full((ens, lane_half), foot_ref[b % foot, b // foot], jnp.int32) for b in range(blocks)]
            for slot, peer in enumerate(src_peers + [my_src]):
                total = tree([jnp.where(names[b] == peer, outs[b], 0.0) for b in range(blocks)])
                if slot < n_src - 1:
                    terms[slot] = total
                    copy(terms.at[slot], arrived.at[my_src], z_send, z_recv, {"src": peer})
                else:
                    arrived[my_src] = total

        def scatter_finish():
            drain(arrived, z_recv, n_src)
            return sum_of(arrived, n_src)

        def gather_start(value, dst):
            field[0] = value
            for peer in src_peers:
                copy(field.at[0], dst.at[my_src], f_send, f_recv, {"src": peer})
            dst[my_src] = value

        def adjoint_terms(src, dst):
            for s in range(src_dev):
                total = None
                for f in range(foot):
                    x = src[foot_ref[f, s]]
                    x = jnp.concatenate([jnp.where(upper, x, 0.0), jnp.where(upper, 0.0, x)], axis=1)
                    out = lax.dot_general(
                        jnp.concatenate(split(x), axis=0), w[s * foot + f],
                        (((1,), (1,)), ((), ())), preferred_element_type=F32,
                    )
                    out = out[0:ens] + out[ens:2 * ens]
                    out = out[:, 0:width] + out[:, width:2 * width]
                    total = out if total is None else total + out
                dst[my_gauge, s] = total

        def gauge_start(dst, i):
            for peer in gauge_peers:
                copy(dst.at[my_gauge], dst.at[my_gauge], y_send.at[i], y_recv.at[i], {"gauge": peer})

        def gauge_finish(dst, i):
            drain(dst, y_recv.at[i], n_gauge)
            total = sum_of(dst, n_gauge)
            return jnp.stack([total[s] + swap(total[s]) for s in range(src_dev)])

        def rows_start(row, dst, i):
            rows_out[i] = row
            for peer in src_peers:
                copy(rows_out.at[i], dst.at[my_src], r_send.at[i], r_recv.at[i], {"src": peer})
            dst[my_src] = row

        def rows_finish(dst, i):
            drain(dst, r_recv.at[i], n_src)
            return sum_of(dst, n_src)

        def plane_start(row, dst, i):
            rows_out[2 + i] = row
            for peer in plane_peers:
                copy(rows_out.at[2 + i], dst.at[my_plane], p_send.at[i], p_recv.at[i], peer)
            dst[my_plane] = row

        def plane_finish(dst, i):
            drain(dst, p_recv.at[i], n_plane)
            return sum_of(dst, n_plane)

        both = [theta0[s] for s in range(src_dev)]
        if h == 0:
            theta = jnp.stack([jnp.where(upper, t, swap(t)) for t in both])
        else:
            theta = jnp.stack([jnp.where(upper, swap(t), t) for t in both])

        for outer in range(GN_STEPS):
            slope = jax.nn.sigmoid(theta)
            coef = jnp.maximum(theta, 0.0) + jnp.log1p(jnp.exp(-jnp.abs(theta)))
            outs = products(coef)
            if outer == 0 and h == 0:
                pl.semaphore_wait(barrier, n_src + n_plane - 2)
            scatter_start(outs)
            yield

            if outer == 0 and h == 0:
                loads[2 + src_dev].wait()
            first, second = obs[:, 0:lane_half], obs[:, lane_half:]
            seen = jnp.where(upper, first, swap(second)) if h == 0 else jnp.where(upper, swap(first), second)
            misfit = scatter_finish() - seen
            gather_start(misfit, gathered_m)
            results["misfit", h] = misfit
            drain(terms, z_send, n_src)
            yield

            drain(gathered_m, f_recv, n_src)
            adjoint_terms(gathered_m, adj_g)
            gauge_start(adj_g, 0)
            drain(gathered_m, f_send, n_src)
            yield

            d0 = -(slope * gauge_finish(adj_g, 0) + DAMPING * theta)
            scatter_start(products(slope * d0))
            rows_start(to_row([inner(d0, d0)]), rows_in, 0)
            drain(adj_g, y_send.at[0], n_gauge)
            yield

            b0 = scatter_finish()
            gather_start(b0, gathered_b)
            drain(terms, z_send, n_src)
            yield

            drain(gathered_b, f_recv, n_src)
            adjoint_terms(gathered_b, adj_p)
            gauge_start(adj_p, 1)
            rr_row = rows_finish(rows_in, 0)
            drain(rows_in, r_send.at[0], n_src)
            squares = tree([gathered_b[t] * gathered_b[t] for t in range(n_src)])
            bb_row = to_row([jnp.sum(squares, axis=1, keepdims=True)])
            plane_start(bb_row + jnp.where(lanes[0:1] < half, 0.0, pltpu.roll(rr_row, half, 1)), plane_a, 0)
            drain(gathered_b, f_send, n_src)
            yield

            p = slope * gauge_finish(adj_p, 1) + DAMPING * d0
            scatter_start(products(slope * p))
            drain(adj_p, y_send.at[1], n_gauge)
            yield

            row = plane_finish(plane_a, 0)
            bb, rr0 = from_row(row, 0), from_row(row, 1) * (1.0 / n_gauge)
            alpha0 = rr0 / (bb + DAMPING * rr0)
            res = d0 - alpha0[None] * p
            rr1, rd = inner(res, res), inner(res, d0)
            drain(plane_a, p_send.at[0], n_plane)
            image = b0 - alpha0 * scatter_finish()
            rows_start(to_row([inner_tile(image, image), inner_tile(image, b0), rr1, rd]), scal_in, 1)
            drain(terms, z_send, n_src)
            yield

            plane_start(rows_finish(scal_in, 1), plane_b, 1)
            drain(scal_in, r_send.at[1], n_src)
            yield

            row = plane_finish(plane_b, 1)
            cc, cb = from_row(row, 0), from_row(row, 1)
            rr1, rd = from_row(row, 2) * (1.0 / n_gauge), from_row(row, 3) * (1.0 / n_gauge)
            beta = rr1 / rr0
            curv = cc + beta * (2.0 * cb + beta * bb) + DAMPING * (rr1 + beta * (2.0 * rd + beta * rr0))
            alpha1 = rr1 / curv
            theta = theta + (alpha0[None] * d0 + alpha1[None] * (res + beta[None] * d0))
            drain(plane_b, p_send.at[1], n_plane)
        results["theta", h] = theta

    loads[0].wait()
    loads[1].wait()
    for b in range(blocks):
        if b % foot == 0:
            loads[2 + b // foot].wait()
        hi, lo = split(raw[b])
        w[b, 0:width, :] = hi
        w[b, width:2 * width, :] = lo

    each = len(scratch) // 2
    running = [chain(h, scratch[h * each:(h + 1) * each]) for h in range(2)]
    while running:
        running = [c for c in running if next(c, True) is None]

    for s in range(src_dev):
        theta_ref[s] = jnp.where(upper, results["theta", 0][s], results["theta", 1][s])
    one, two = results["misfit", 0], results["misfit", 1]
    misfit_ref[:, 0:lane_half] = jnp.where(upper, one, swap(two))
    misfit_ref[:, lane_half:] = jnp.where(upper, swap(one), two)


def hand_over(theta_in, misfit_in, theta_out, misfit_out):
    theta_out[...] = theta_in[...]
    misfit_out[...] = misfit_in[...]


def local(sizes, responses, footprint, theta_start, observed):
    n_src, n_tile, n_gauge = sizes
    src_dev, foot, _, width, length = responses.shape
    ens = theta_start.shape[1]
    blocks = src_dev * foot
    vmem, anywhere = pl.BlockSpec(memory_space=pltpu.VMEM), pl.BlockSpec(memory_space=pl.ANY)
    dma = pltpu.SemaphoreType.DMA
    row, packed = (1, 128), (ens, length // 2)
    theta, misfit = pl.pallas_call(
        functools.partial(kernel, (n_src, n_tile, n_gauge, src_dev, foot)),
        out_shape=(
            jax.ShapeDtypeStruct(theta_start.shape, F32),
            jax.ShapeDtypeStruct((ens, length), F32),
        ),
        in_specs=[anywhere] * 4,
        out_specs=(vmem, vmem),
        scratch_shapes=[
            pltpu.VMEM((blocks, width, length), F32),
            pltpu.VMEM((blocks, 2 * width, length), BF16),
            pltpu.SMEM((foot, src_dev), jnp.int32),
            pltpu.VMEM((src_dev, ens, width), F32),
            pltpu.VMEM((ens, length), F32),
            dma((3 + src_dev,)),
        ] + 2 * [
            pltpu.VMEM((n_src - 1,) + packed, F32),
            pltpu.VMEM((n_src,) + packed, F32),
            pltpu.VMEM((1,) + packed, F32),
            pltpu.VMEM((n_src,) + packed, F32),
            pltpu.VMEM((n_src,) + packed, F32),
            pltpu.VMEM((n_gauge, src_dev, ens, width), F32),
            pltpu.VMEM((n_gauge, src_dev, ens, width), F32),
            pltpu.VMEM((4,) + row, F32),
            pltpu.VMEM((n_src,) + row, F32),
            pltpu.VMEM((n_src,) + row, F32),
            pltpu.VMEM((n_tile * n_gauge,) + row, F32),
            pltpu.VMEM((n_tile * n_gauge,) + row, F32),
            dma, dma, dma, dma,
            dma((2,)), dma((2,)), dma((2,)), dma((2,)), dma((2,)), dma((2,)),
        ],
        compiler_params=pltpu.CompilerParams(collective_id=0, has_side_effects=True),
    )(
        responses.reshape(blocks, width, length),
        footprint.T,
        theta_start,
        observed.reshape(ens, length),
    )
    theta, misfit = pl.pallas_call(
        hand_over,
        out_shape=(
            jax.ShapeDtypeStruct(theta_start.shape, F32),
            jax.ShapeDtypeStruct((ens, length), F32),
        ),
        in_specs=[vmem, vmem],
        out_specs=(vmem, vmem),
    )(theta, misfit)
    return theta, misfit.reshape(observed.shape)


def solution(mesh):
    sizes = (mesh.shape["src"], mesh.shape["tile"], mesh.shape["gauge"])
    in_specs = (
        P(("src", "tile"), None, "gauge", None, None),
        P(("src", "tile"), None),
        P(("src", "tile"), None, None),
        P(("src", "tile"), "gauge", None, None),
    )
    out_specs = (P(("src", "tile"), None, None), P(("src", "tile"), "gauge", None, None))
    return jax.shard_map(
        functools.partial(local, sizes), mesh=mesh, in_specs=in_specs, out_specs=out_specs, check_vma=False
    )
```

```python
import functools

import jax
import jax.numpy as jnp
from jax import lax
from jax.experimental import pallas as pl
from jax.experimental.pallas import tpu as pltpu
from jax.sharding import PartitionSpec as P

GN_STEPS = 2
DAMPING = 0.1
MESH = pl.DeviceIdType.MESH
F32 = jnp.float32
BF16 = jnp.bfloat16


def split(x):
    hi = x.astype(BF16)
    return hi, (x - hi.astype(F32)).astype(BF16)


def far_first(n):
    return sorted(range(1, n), key=lambda j: (-min(j, n - j), j))


def kernel(
    sizes,
    resp_hbm, foot_hbm, theta_hbm, obs_hbm,
    theta_ref, misfit_ref,
    raw, w, foot_ref, theta0, obs, load_sem, *scratch,
):
    n_src, n_tile, n_gauge, src_dev, foot = sizes
    blocks = src_dev * foot
    ens, width = theta0.shape[1:]
    half, lane_half = ens // 2, obs.shape[1] // 2
    my_src, my_tile, my_gauge = lax.axis_index("src"), lax.axis_index("tile"), lax.axis_index("gauge")

    src_peers = [lax.rem(my_src + j, n_src) for j in far_first(n_src)]
    gauge_peers = [lax.rem(my_gauge + j, n_gauge) for j in far_first(n_gauge)]

    def hops(ab):
        a, b = ab[0] // 2, ab[1]
        return -(min(a, n_tile // 2 - a) + min(b, n_gauge - b))

    plane_peers = [
        {"tile": lax.rem(my_tile + a, n_tile), "gauge": lax.rem(my_gauge + b, n_gauge)}
        for a, b in sorted([(a, b) for a in range(n_tile) for b in range(n_gauge) if a or b], key=hops)
    ]
    my_plane = my_tile * n_gauge + my_gauge
    n_plane = n_tile * n_gauge

    loads = [
        pltpu.make_async_copy(a, b, load_sem.at[i])
        for i, (a, b) in enumerate(
            [(theta_hbm, theta0), (foot_hbm, foot_ref)]
            + [(resp_hbm.at[pl.ds(s * foot, foot)], raw.at[pl.ds(s * foot, foot)]) for s in range(src_dev)]
            + [(obs_hbm, obs)]
        )
    ]
    for load in loads:
        load.start()

    barrier = pltpu.get_barrier_semaphore()
    for peer in [{"src": p} for p in src_peers] + plane_peers:
        pl.semaphore_signal(barrier, inc=1, device_id=peer, device_id_type=MESH)

    lanes = lax.broadcasted_iota(jnp.int32, (ens, 128), 1)
    sub = lax.broadcasted_iota(jnp.int32, (ens, 128), 0)
    upper = sub < half
    place = jnp.where(upper, sub, sub - half)

    def swap(x):
        return pltpu.roll(x, half, 0)

    def to_row(values):
        out = jnp.zeros((ens, 128), F32)
        for i, v in enumerate(values):
            out = out + jnp.where(lanes == place + i * half, v, 0.0)
        return jnp.sum(out, axis=0, keepdims=True)

    def from_row(row, i):
        return jnp.sum(jnp.where(lanes == place + i * half, row, 0.0), axis=1, keepdims=True)

    def copy(src, dst, send_sem, recv_sem, peer):
        pltpu.make_async_remote_copy(
            src_ref=src, dst_ref=dst, send_sem=send_sem, recv_sem=recv_sem,
            device_id=peer, device_id_type=MESH,
        ).start()

    def drain(ref, sem, n):
        part = ref.at[pl.ds(0, n - 1)]
        pltpu.make_async_copy(part, part, sem).wait()

    def tree(parts):
        while len(parts) > 1:
            parts = [sum(parts[i:i + 2]) for i in range(0, len(parts), 2)]
        return parts[0]

    def sum_of(ref, n):
        return tree([ref[i] for i in range(n)])

    def inner(a, b):
        return 0.5 * jnp.sum(tree([a[s] * b[s] for s in range(src_dev)]), axis=1, keepdims=True)

    def inner_tile(a, b):
        return jnp.sum(a * b, axis=1, keepdims=True)

    def products(x):
        outs = []
        for s in range(src_dev):
            hi, lo = split(x[s])
            left = jnp.concatenate(
                [jnp.concatenate([hi, hi], axis=1), jnp.concatenate([lo, lo], axis=1)], axis=0
            )
            for f in range(foot):
                out = jnp.dot(left, w[s * foot + f], preferred_element_type=F32)
                out = out[0:ens] + out[ens:2 * ens]
                outs.append(jnp.where(upper, out[:, 0:lane_half], out[:, lane_half:]))
        return outs

    results = {}

    def chain(h, refs):
        (
            terms, arrived, field, gathered_m, gathered_b, adj_g, adj_p,
            rows_out, rows_in, scal_in, plane_a, plane_b,
            z_send, z_recv, f_send, f_recv, y_send, y_recv, r_send, r_recv, p_send, p_recv,
        ) = refs

        def scatter_start(outs):
            names = [jnp.full((ens, lane_half), foot_ref[b % foot, b // foot], jnp.int32) for b in range(blocks)]
            for slot, peer in enumerate(src_peers + [my_src]):
                total = tree([jnp.where(names[b] == peer, outs[b], 0.0) for b in range(blocks)])
                if slot < n_src - 1:
                    terms[slot] = total
                    copy(terms.at[slot], arrived.at[my_src], z_send, z_recv, {"src": peer})
                else:
                    arrived[my_src] = total

        def scatter_finish():
            drain(arrived, z_recv, n_src)
            return sum_of(arrived, n_src)

        def gather_start(value, dst):
            field[0] = value
            for peer in src_peers:
                copy(field.at[0], dst.at[my_src], f_send, f_recv, {"src": peer})
            dst[my_src] = value

        def adjoint_terms(src, dst):
            sums = []
            for s in range(src_dev):
                total = None
                for f in range(foot):
                    x = src[foot_ref[f, s]]
                    x = jnp.concatenate([jnp.where(upper, x, 0.0), jnp.where(upper, 0.0, x)], axis=1)
                    out = lax.dot_general(
                        jnp.concatenate(split(x), axis=0), w[s * foot + f],
                        (((1,), (1,)), ((), ())), preferred_element_type=F32,
                    )
                    out = out[0:ens] + out[ens:2 * ens]
                    out = out[:, 0:width] + out[:, width:2 * width]
                    total = out if total is None else total + out
                sums.append(total + swap(total))
            for pair in range(src_dev // 2):
                dst[my_gauge, pair] = jnp.where(upper, sums[2 * pair], sums[2 * pair + 1])

        def gauge_start(dst, i):
            for peer in gauge_peers:
                copy(dst.at[my_gauge], dst.at[my_gauge], y_send.at[i], y_recv.at[i], {"gauge": peer})

        def gauge_finish(dst, i):
            drain(dst, y_recv.at[i], n_gauge)
            total = sum_of(dst, n_gauge)
            out = []
            for pair in range(src_dev // 2):
                turned = swap(total[pair])
                out += [jnp.where(upper, total[pair], turned), jnp.where(upper, turned, total[pair])]
            return jnp.stack(out)

        def rows_start(row, dst, i):
            rows_out[i] = row
            for peer in src_peers:
                copy(rows_out.at[i], dst.at[my_src], r_send.at[i], r_recv.at[i], {"src": peer})
            dst[my_src] = row

        def rows_finish(dst, i):
            drain(dst, r_recv.at[i], n_src)
            return sum_of(dst, n_src)

        def plane_start(row, dst, i):
            rows_out[2 + i] = row
            for peer in plane_peers:
                copy(rows_out.at[2 + i], dst.at[my_plane], p_send.at[i], p_recv.at[i], peer)
            dst[my_plane] = row

        def plane_finish(dst, i):
            drain(dst, p_recv.at[i], n_plane)
            return sum_of(dst, n_plane)

        both = [theta0[s] for s in range(src_dev)]
        if h == 0:
            theta = jnp.stack([jnp.where(upper, t, swap(t)) for t in both])
        else:
            theta = jnp.stack([jnp.where(upper, swap(t), t) for t in both])

        for outer in range(GN_STEPS):
            slope = jax.nn.sigmoid(theta)
            coef = jnp.maximum(theta, 0.0) + jnp.log1p(jnp.exp(-jnp.abs(theta)))
            outs = products(coef)
            if outer == 0 and h == 0:
                pl.semaphore_wait(barrier, n_src + n_plane - 2)
            scatter_start(outs)
            yield

            if outer == 0 and h == 0:
                loads[2 + src_dev].wait()
            first, second = obs[:, 0:lane_half], obs[:, lane_half:]
            seen = jnp.where(upper, first, swap(second)) if h == 0 else jnp.where(upper, swap(first), second)
            misfit = scatter_finish() - seen
            gather_start(misfit, gathered_m)
            results["misfit", h] = misfit
            drain(terms, z_send, n_src)
            yield

            drain(gathered_m, f_recv, n_src)
            adjoint_terms(gathered_m, adj_g)
            gauge_start(adj_g, 0)
            drain(gathered_m, f_send, n_src)
            yield

            d0 = -(slope * gauge_finish(adj_g, 0) + DAMPING * theta)
            scatter_start(products(slope * d0))
            yield

            rows_start(to_row([inner(d0, d0)]), rows_in, 0)
            drain(adj_g, y_send.at[0], n_gauge)
            yield

            b0 = scatter_finish()
            gather_start(b0, gathered_b)
            drain(terms, z_send, n_src)
            yield

            drain(gathered_b, f_recv, n_src)
            adjoint_terms(gathered_b, adj_p)
            gauge_start(adj_p, 1)
            yield

            rr_row = rows_finish(rows_in, 0)
            drain(rows_in, r_send.at[0], n_src)
            squares = tree([gathered_b[t] * gathered_b[t] for t in range(n_src)])
            bb_row = to_row([jnp.sum(squares, axis=1, keepdims=True)])
            plane_start(bb_row + jnp.where(lanes[0:1] < half, 0.0, pltpu.roll(rr_row, half, 1)), plane_a, 0)
            drain(gathered_b, f_send, n_src)
            yield

            p = slope * gauge_finish(adj_p, 1) + DAMPING * d0
            scatter_start(products(slope * p))
            drain(adj_p, y_send.at[1], n_gauge)
            yield

            row = plane_finish(plane_a, 0)
            bb, rr0 = from_row(row, 0), from_row(row, 1) * (1.0 / n_gauge)
            alpha0 = rr0 / (bb + DAMPING * rr0)
            res = d0 - alpha0[None] * p
            rr1, rd = inner(res, res), inner(res, d0)
            drain(plane_a, p_send.at[0], n_plane)
            image = b0 - alpha0 * scatter_finish()
            rows_start(to_row([inner_tile(image, image), inner_tile(image, b0), rr1, rd]), scal_in, 1)
            drain(terms, z_send, n_src)
            yield

            plane_start(rows_finish(scal_in, 1), plane_b, 1)
            drain(scal_in, r_send.at[1], n_src)
            yield

            row = plane_finish(plane_b, 1)
            cc, cb = from_row(row, 0), from_row(row, 1)
            rr1, rd = from_row(row, 2) * (1.0 / n_gauge), from_row(row, 3) * (1.0 / n_gauge)
            beta = rr1 / rr0
            curv = cc + beta * (2.0 * cb + beta * bb) + DAMPING * (rr1 + beta * (2.0 * rd + beta * rr0))
            alpha1 = rr1 / curv
            theta = theta + (alpha0[None] * d0 + alpha1[None] * (res + beta[None] * d0))
            drain(plane_b, p_send.at[1], n_plane)
        results["theta", h] = theta

    loads[0].wait()
    loads[1].wait()
    for b in range(blocks):
        if b % foot == 0:
            loads[2 + b // foot].wait()
        hi, lo = split(raw[b])
        w[b, 0:width, :] = hi
        w[b, width:2 * width, :] = lo

    each = len(scratch) // 2
    running = [chain(h, scratch[h * each:(h + 1) * each]) for h in range(2)]
    while running:
        running = [c for c in running if next(c, True) is None]

    for s in range(src_dev):
        theta_ref[s] = jnp.where(upper, results["theta", 0][s], results["theta", 1][s])
    one, two = results["misfit", 0], results["misfit", 1]
    misfit_ref[:, 0:lane_half] = jnp.where(upper, one, swap(two))
    misfit_ref[:, lane_half:] = jnp.where(upper, swap(one), two)


def hand_over(theta_in, misfit_in, theta_out, misfit_out):
    theta_out[...] = theta_in[...]
    misfit_out[...] = misfit_in[...]


def local(sizes, responses, footprint, theta_start, observed):
    n_src, n_tile, n_gauge = sizes
    src_dev, foot, _, width, length = responses.shape
    ens = theta_start.shape[1]
    blocks = src_dev * foot
    vmem, anywhere = pl.BlockSpec(memory_space=pltpu.VMEM), pl.BlockSpec(memory_space=pl.ANY)
    dma = pltpu.SemaphoreType.DMA
    row, packed = (1, 128), (ens, length // 2)
    theta, misfit = pl.pallas_call(
        functools.partial(kernel, (n_src, n_tile, n_gauge, src_dev, foot)),
        out_shape=(
            jax.ShapeDtypeStruct(theta_start.shape, F32),
            jax.ShapeDtypeStruct((ens, length), F32),
        ),
        in_specs=[anywhere] * 4,
        out_specs=(vmem, vmem),
        scratch_shapes=[
            pltpu.VMEM((blocks, width, length), F32),
            pltpu.VMEM((blocks, 2 * width, length), BF16),
            pltpu.SMEM((foot, src_dev), jnp.int32),
            pltpu.VMEM((src_dev, ens, width), F32),
            pltpu.VMEM((ens, length), F32),
            dma((3 + src_dev,)),
        ] + 2 * [
            pltpu.VMEM((n_src - 1,) + packed, F32),
            pltpu.VMEM((n_src,) + packed, F32),
            pltpu.VMEM((1,) + packed, F32),
            pltpu.VMEM((n_src,) + packed, F32),
            pltpu.VMEM((n_src,) + packed, F32),
            pltpu.VMEM((n_gauge, src_dev // 2, ens, width), F32),
            pltpu.VMEM((n_gauge, src_dev // 2, ens, width), F32),
            pltpu.VMEM((4,) + row, F32),
            pltpu.VMEM((n_src,) + row, F32),
            pltpu.VMEM((n_src,) + row, F32),
            pltpu.VMEM((n_tile * n_gauge,) + row, F32),
            pltpu.VMEM((n_tile * n_gauge,) + row, F32),
            dma, dma, dma, dma,
            dma((2,)), dma((2,)), dma((2,)), dma((2,)), dma((2,)), dma((2,)),
        ],
        compiler_params=pltpu.CompilerParams(collective_id=0, has_side_effects=True),
    )(
        responses.reshape(blocks, width, length),
        footprint.T,
        theta_start,
        observed.reshape(ens, length),
    )
    theta, misfit = pl.pallas_call(
        hand_over,
        out_shape=(
            jax.ShapeDtypeStruct(theta_start.shape, F32),
            jax.ShapeDtypeStruct((ens, length), F32),
        ),
        in_specs=[vmem, vmem],
        out_specs=(vmem, vmem),
    )(theta, misfit)
    return theta, misfit.reshape(observed.shape)


def solution(mesh):
    sizes = (mesh.shape["src"], mesh.shape["tile"], mesh.shape["gauge"])
    in_specs = (
        P(("src", "tile"), None, "gauge", None, None),
        P(("src", "tile"), None),
        P(("src", "tile"), None, None),
        P(("src", "tile"), "gauge", None, None),
    )
    out_specs = (P(("src", "tile"), None, None), P(("src", "tile"), "gauge", None, None))
    return jax.shard_map(
        functools.partial(local, sizes), mesh=mesh, in_specs=in_specs, out_specs=out_specs, check_vma=False
    )
```
